32 devices in a mesh: gx: 2 (over y), gy: 4 (over x, core), gz: 4 (over z).
Axes of the slice: x: 2, y: 2, z: 4, core: 2. Of those that a mesh axis runs over, the one named last changes fastest.
Arguments:
- velocity: float32 [3, 64, 128, 512], P(None, 'gx', 'gy', 'gz'), may hold values from -3 to 3
- box_level: float32 [512, 16, 256], P(('gx', 'gy', 'gz')), may hold values from -9 to 9
- corners: int32 [512, 3], P(('gx', 'gy', 'gz')), may hold values from 0 to 112, as said below
- owner_list: int32 [512], P(('gx', 'gy', 'gz')), may hold values from -1 to 15, as said below
Outputs:
- new_velocity: float32 [3, 64, 128, 512], P(None, 'gx', 'gy', 'gz')
- level_sets: float32 [512, 16, 256], P(('gx', 'gy', 'gz'))
- curvature: float32 [512, 16, 256], P(('gx', 'gy', 'gz'))
The draws below stay inside these ranges and needn't reach their ends.
Inputs may be any that keep to these rules, and one draw needn't show every extreme that they name: `owner_list`: -1 marks an empty slot. The live slots of one device name different helpers, numbered in the order of the devices of its gy+gz group (gy slowest) at the device's own index along gx; every helper is named by exactly 8 slots of its group; a device has 0 to 16 live slots, and some device of every group has 16. `corners`: columns 0, 1, 2 lie in 0 to 16, 16, 112: every box lies inside its home device's block. Boxes may intersect.
All inputs are finite; a program needn't handle non-finite values.
Results may differ from the reference program's by a relative error of at most 0.0003.
Values sent between devices are 32-bit elements; how exact they have to be, the bound alone decides.
A program may use at most 128 MiB of HBM per device.

```python
import math
import jax
import jax.numpy as jnp
from jax import lax

CX = 32
CY = 32
CZ = 128
BOX = 16
ITERS = 12
GROUP = 16
HELP = 8
SLOTS = 16
SLOTS_ALL = 512
NX = 64
NY = 128
NZ = 512
N_GY = 4
N_GZ = 4


def draw_corners(key, part):
    along_x = jax.random.randint(jax.random.fold_in(key, 11), (SLOTS_ALL, 1), 0, CX - BOX + 1)
    along_y = jax.random.randint(jax.random.fold_in(key, 13), (SLOTS_ALL, 1), 0, CY - BOX + 1)
    along_z = jax.random.randint(jax.random.fold_in(key, 17), (SLOTS_ALL, 1), 0, CZ - BOX + 1)
    return jnp.concatenate([along_x, along_y, along_z], axis=1).astype(jnp.int32)


def group_owners(group_key):
    pair_count = GROUP // 2
    subkeys = jax.random.split(group_key, 4)
    excess = jax.random.randint(subkeys[0], (pair_count,), 0, HELP + 1)
    excess = excess.at[0].set(HELP)
    counts = jnp.concatenate([HELP + excess, HELP - excess])
    counts = counts[jax.random.permutation(subkeys[1], GROUP)]
    starts = jnp.cumsum(counts) - counts
    relabel = jax.random.permutation(subkeys[2], GROUP).astype(jnp.int32)
    position = jnp.arange(SLOTS, dtype=jnp.int32)
    serial = starts[:, None] + position[None, :]
    named_ids = jnp.where(position[None, :] < counts[:, None], relabel[serial % GROUP], -1)
    home_keys = jax.random.split(subkeys[3], GROUP)
    orders = jax.vmap(lambda home_key: jax.random.permutation(home_key, SLOTS))(home_keys)
    return jnp.take_along_axis(named_ids, orders, axis=1)


def draw_owner_list(key, part):
    group_keys = jax.random.split(jax.random.fold_in(key, 29), SLOTS_ALL // (SLOTS * GROUP))
    owners = jax.vmap(group_owners)(group_keys)
    return owners.reshape(SLOTS_ALL).astype(jnp.int32)


def shard_levels(stream_key, dims, pieces, smallest, largest):
    loudness, own = 1.0, jax.random.fold_in(stream_key, 6)
    for dim, parts in pieces:
        heights = jnp.exp(jax.random.uniform(jax.random.fold_in(own, dim), (parts,), jnp.float32, smallest / len(pieces), largest / len(pieces)))
        loudness = loudness * jnp.repeat(heights, dims[dim] // parts).reshape([-1 if axis == dim else 1 for axis in range(len(dims))])
    return loudness


def centred(own_key, dims, deviation, limit, shards=(), kind=jnp.bfloat16):
    factor_of = shard_levels(own_key, dims, shards, -0.22, 0.18) if shards else 1.0
    array = jax.random.normal(own_key, dims, jnp.float32) * deviation * factor_of
    return jnp.minimum(jnp.maximum(array, -limit), limit).astype(kind)


def setup_inputs(seed: int = 0) -> dict:
    splits = jax.random.split(jax.random.key(seed), 5)
    velocity = centred(splits[0], (3, NX, NY, NZ), 0.5, 3.0, ((1, 2), (2, 4), (3, 4)), jnp.float32)
    box_level = centred(splits[1], (SLOTS_ALL, BOX, BOX * BOX), 1.5, 9.0, ((0, 32),), jnp.float32)
    corners = draw_corners(jax.random.fold_in(splits[4], 71), 0)
    owner_list = draw_owner_list(jax.random.fold_in(splits[4], 71), 0)
    return {"velocity": velocity, "box_level": box_level, "corners": corners, "owner_list": owner_list}


box_step = 0.25
pseudo_step = 0.3
weno_floor = 1e-06
band_width = 1.5
tension = 2.0
grid_step = 0.2
viscosity = 0.1
normal_floor = 0.5

def neighbour(values, across, forward):
    length = values.shape[-2]
    plane_size = values.shape[-1]
    if across == 0:
        if forward:
            return jnp.concatenate([values[..., 1:, :], values[..., -1:, :]], axis=-2)
        return jnp.concatenate([values[..., :1, :], values[..., :-1, :]], axis=-2)
    stride = length if across == 1 else 1
    places = jnp.arange(plane_size, dtype=jnp.int32)
    column = places // length if across == 1 else places % length
    if forward:
        shifted = jnp.concatenate([values[..., stride:], values[..., :stride]], axis=-1)
        return jnp.where(column == length - 1, values, shifted)
    shifted = jnp.concatenate([values[..., plane_size - stride:], values[..., :plane_size - stride]], axis=-1)
    return jnp.where(column == 0, values, shifted)

def weno_blend(slope_one, slope_two, slope_three, slope_four, slope_five):
    smooth_one = 13.0 / 12.0 * (slope_one - 2.0 * slope_two + slope_three) ** 2 + 0.25 * (slope_one - 4.0 * slope_two + 3.0 * slope_three) ** 2
    smooth_two = 13.0 / 12.0 * (slope_two - 2.0 * slope_three + slope_four) ** 2 + 0.25 * (slope_two - slope_four) ** 2
    smooth_three = 13.0 / 12.0 * (slope_three - 2.0 * slope_four + slope_five) ** 2 + 0.25 * (3.0 * slope_three - 4.0 * slope_four + slope_five) ** 2
    weight_one = 0.1 / (weno_floor + smooth_one) ** 2
    weight_two = 0.6 / (weno_floor + smooth_two) ** 2
    weight_three = 0.3 / (weno_floor + smooth_three) ** 2
    poly_one = slope_one / 3.0 - 7.0 * slope_two / 6.0 + 11.0 * slope_three / 6.0
    poly_two = -slope_two / 6.0 + 5.0 * slope_three / 6.0 + slope_four / 3.0
    poly_three = slope_three / 3.0 + 5.0 * slope_four / 6.0 - slope_five / 6.0
    return (weight_one * poly_one + weight_two * poly_two + weight_three * poly_three) / (weight_one + weight_two + weight_three)

def upwind_slopes(values, across):
    behind = values - neighbour(values, across, False)
    back_one = neighbour(behind, across, False)
    back_two = neighbour(back_one, across, False)
    ahead_one = neighbour(behind, across, True)
    ahead_two = neighbour(ahead_one, across, True)
    ahead_three = neighbour(ahead_two, across, True)
    minus_side = weno_blend(back_two, back_one, behind, ahead_one, ahead_two)
    plus_side = weno_blend(ahead_three, ahead_two, ahead_one, behind, back_one)
    return (minus_side, plus_side)

def central_slopes(values):
    return [0.5 * (neighbour(values, across, True) - neighbour(values, across, False)) for across in range(3)]

def evolve_boxes(levels, motion):
    change = jnp.zeros_like(levels)
    for across in range(3):
        minus_side, plus_side = upwind_slopes(levels, across)
        speed_d = motion[:, across]
        change = change + jnp.maximum(speed_d, 0.0) * minus_side + jnp.minimum(speed_d, 0.0) * plus_side
    advected = levels - box_step * change
    sign_soft = advected / jnp.sqrt(advected * advected + 1.0)
    outside = advected > 0.0

    def one_sweep(counter, current):
        squared = jnp.zeros_like(current)
        for across in range(3):
            behind = current - neighbour(current, across, False)
            ahead_d = neighbour(current, across, True) - current
            upper_sq = jnp.maximum(jnp.maximum(behind, 0.0) ** 2, jnp.minimum(ahead_d, 0.0) ** 2)
            lower_sq = jnp.maximum(jnp.minimum(behind, 0.0) ** 2, jnp.maximum(ahead_d, 0.0) ** 2)
            squared = squared + jnp.where(outside, upper_sq, lower_sq)
        return current - pseudo_step * sign_soft * (jnp.sqrt(squared) - 1.0)
    settled = lax.fori_loop(0, ITERS, one_sweep, advected)
    slopes = central_slopes(settled)
    magnitude = jnp.maximum(jnp.sqrt(slopes[0] ** 2 + slopes[1] ** 2 + slopes[2] ** 2), normal_floor)
    bending = jnp.zeros_like(settled)
    for across in range(3):
        unit_d = slopes[across] / magnitude
        bending = bending + 0.5 * (neighbour(unit_d, across, True) - neighbour(unit_d, across, False))
    return (settled, bending)

def surface_force(levels, bending):
    slopes = central_slopes(levels)
    delta_band = jnp.exp(-(levels / band_width) ** 2) / (band_width * math.sqrt(math.pi))
    strength = tension * bending * delta_band
    return jnp.stack([strength * slopes[0], strength * slopes[1], strength * slopes[2]], axis=1)

def tendency(padded):
    centre = padded[:, 1:-1, 1:-1, 1:-1]
    uppers = (padded[:, 2:, 1:-1, 1:-1], padded[:, 1:-1, 2:, 1:-1], padded[:, 1:-1, 1:-1, 2:])
    lowers = (padded[:, :-2, 1:-1, 1:-1], padded[:, 1:-1, :-2, 1:-1], padded[:, 1:-1, 1:-1, :-2])
    advect = jnp.zeros_like(centre)
    spread = -6.0 * centre
    for across in range(3):
        advect = advect + centre[across:across + 1] * (uppers[across] - lowers[across]) * 0.5
        spread = spread + uppers[across] + lowers[across]
    return viscosity * spread - advect

def wrap_pad(values):
    return jnp.pad(values, ((0, 0), (1, 1), (1, 1), (1, 1)), mode='wrap')

def reference(velocity, box_level, corners, owner_list):
    alive_mask = (owner_list >= 0).astype(jnp.float32)
    slot_ids = jnp.arange(SLOTS_ALL, dtype=jnp.int32)
    device = slot_ids // SLOTS
    anchor_x = (device // (N_GY * N_GZ) * CX + corners[:, 0]).astype(jnp.int32)
    anchor_y = (device // N_GZ % N_GY * CY + corners[:, 1]).astype(jnp.int32)
    anchor_z = (device % N_GZ * CZ + corners[:, 2]).astype(jnp.int32)
    nought = jnp.zeros((), jnp.int32)

    def one_box(packed):
        level_box, place_x, place_y, place_z = packed
        motion = lax.dynamic_slice(velocity, (nought, place_x, place_y, place_z), (3, BOX, BOX, BOX))
        motion = motion.reshape(1, 3, BOX, BOX * BOX)
        settled, bending = evolve_boxes(level_box[None], motion)
        return (settled[0], bending[0])
    settled, bending = lax.map(one_box, (box_level, anchor_x, anchor_y, anchor_z))
    settled = settled * alive_mask[:, None, None]
    bending = bending * alive_mask[:, None, None]
    predictor = velocity + grid_step * tendency(wrap_pad(velocity))
    second = predictor + grid_step * tendency(wrap_pad(predictor))
    stepped = 0.5 * (velocity + second)

    def deposit(slot_no, grid_now):
        push_box = surface_force(settled[slot_no][None], bending[slot_no][None])[0].reshape(3, BOX, BOX, BOX)
        corner_at = (nought, anchor_x[slot_no], anchor_y[slot_no], anchor_z[slot_no])
        region = lax.dynamic_slice(grid_now, corner_at, (3, BOX, BOX, BOX))
        return lax.dynamic_update_slice(grid_now, region + grid_step * push_box, corner_at)
    result = lax.fori_loop(0, SLOTS_ALL, deposit, stepped)
    return (result, settled, bending)
```

```python
import functools
import math

import jax
import jax.numpy as jnp
from jax import lax
from jax.experimental import pallas as pl
from jax.experimental.pallas import tpu as pltpu
from jax.sharding import PartitionSpec as P

ITERS = 12

box_step = 0.25
pseudo_step = 0.3
weno_floor = 1e-06
band_width = 1.5
tension = 2.0
grid_step = 0.2
viscosity = 0.1
normal_floor = 0.5
tiny = 1.1754944e-38

MESH = pl.DeviceIdType.MESH


def iota(shape, dim):
    return lax.broadcasted_iota(jnp.int32, shape, dim)


def pack_z(ext, dst, xs, ys, lanes):
    group = iota((ys, lanes), 1) // 4

    def step(x, accs):
        shift = 4 * x + 1
        return tuple(
            jnp.where(group == x, pltpu.roll(ext[c, x + 1], shift, 1), accs[c]) for c in range(3)
        )

    accs = lax.fori_loop(
        0, xs, step, tuple(jnp.zeros((ys, lanes), jnp.float32) for _ in range(3)), unroll=4
    )
    for c in range(3):
        dst[c] = accs[c]


def momentum_kernel(
    sizes, v_hbm, o_ref, ext1, ext2, ysend, yrecv, zsend, zrecv, comb, local_sem, send_sem, recv_sem
):
    _, xs, ys, lanes = v_hbm.shape
    load = pltpu.make_async_copy(v_hbm, ext1.at[:, pl.ds(1, xs)], local_sem)
    load.start()
    ups, downs = [], []
    for axis in ("gx", "gy", "gz"):
        me, n = lax.axis_index(axis), sizes[axis]
        ups.append({axis: lax.rem(me + 1, n)})
        downs.append({axis: lax.rem(me + n - 1, n)})
    barrier = pltpu.get_barrier_semaphore()
    for target in ups + downs:
        pl.semaphore_signal(barrier, inc=1, device_id=target, device_id_type=MESH)
    pl.semaphore_wait(barrier, 6)
    load.wait()

    def exchange(r, ext):
        copies = []

        def send(n, src, dst, target):
            copy = pltpu.make_async_remote_copy(
                src_ref=src,
                dst_ref=dst,
                send_sem=send_sem.at[r, n],
                recv_sem=recv_sem.at[r, n],
                device_id=target,
                device_id_type=MESH,
            )
            copy.start()
            copies.append(copy)

        for c in range(3):
            ysend[r, 0, c] = ext[c, pl.ds(1, xs), ys - 1, :]
            ysend[r, 1, c] = ext[c, pl.ds(1, xs), 0, :]
        pack_z(ext, zsend.at[r], xs, ys, lanes)
        send(0, ext.at[:, xs], ext.at[:, 0], ups[0])
        send(1, ext.at[:, 1], ext.at[:, xs + 1], downs[0])
        send(2, ysend.at[r, 0], yrecv.at[r, 0], ups[1])
        send(3, ysend.at[r, 1], yrecv.at[r, 1], downs[1])
        send(4, zsend.at[r], zrecv.at[r, 0], ups[2])
        send(5, zsend.at[r], zrecv.at[r, 1], downs[2])
        return copies

    lane = iota((ys, lanes), 1)
    row = iota((ys, lanes), 0)
    quarter = lane % 4

    def section(r, ext, emit):
        for c in range(3):
            comb[c] = jnp.where(
                quarter == 0,
                pltpu.roll(zrecv[r, 1, c], lanes - 1, 1),
                pltpu.roll(zrecv[r, 0, c], 1, 1),
            )

        def step(x, carry):
            centre = [ext[c, x + 1] for c in range(3)]
            for c in range(3):
                mid = centre[c]
                x_lo, x_hi = ext[c, x], ext[c, x + 2]
                y_lo = jnp.where(row == 0, yrecv[r, 0, c, pl.ds(x, 1), :], pltpu.roll(mid, 1, 0))
                y_hi = jnp.where(
                    row == ys - 1, yrecv[r, 1, c, pl.ds(x, 1), :], pltpu.roll(mid, ys - 1, 0)
                )
                halo = pltpu.roll(comb[c], lanes - 1 - 4 * x, 1)
                z_lo = jnp.where(lane == 0, halo, pltpu.roll(mid, 1, 1))
                z_hi = jnp.where(lane == lanes - 1, halo, pltpu.roll(mid, lanes - 1, 1))
                spread = (x_hi + x_lo) + (y_hi + y_lo) + (z_hi + z_lo) - 6.0 * mid
                advect = (
                    centre[0] * (x_hi - x_lo) + centre[1] * (y_hi - y_lo) + centre[2] * (z_hi - z_lo)
                )
                emit(c, x, mid + grid_step * (viscosity * spread - 0.5 * advect))
            return carry

        lax.fori_loop(0, xs, step, 0)

    def first(c, x, value):
        ext2[c, x + 1] = value

    def second(c, x, value):
        o_ref[c, x] = 0.5 * (ext1[c, x + 1] + value)

    for copy in exchange(0, ext1):
        copy.wait()
    section(0, ext1, first)
    for copy in exchange(1, ext2):
        copy.wait()
    section(1, ext2, second)


def momentum(velocity):
    sizes = {axis: lax.axis_size(axis) for axis in ("gx", "gy", "gz")}
    _, xs, ys, lanes = velocity.shape
    vmem = pltpu.VMEM
    f32 = jnp.float32
    return pl.pallas_call(
        functools.partial(momentum_kernel, sizes),
        out_shape=jax.ShapeDtypeStruct(velocity.shape, f32),
        in_specs=[pl.BlockSpec(memory_space=pl.ANY)],
        out_specs=pl.BlockSpec(memory_space=pltpu.VMEM),
        scratch_shapes=[
            vmem((3, xs + 2, ys, lanes), f32),
            vmem((3, xs + 2, ys, lanes), f32),
            vmem((2, 2, 3, xs, lanes), f32),
            vmem((2, 2, 3, xs, lanes), f32),
            vmem((2, 3, ys, lanes), f32),
            vmem((2, 2, 3, ys, lanes), f32),
            vmem((3, ys, lanes), f32),
            pltpu.SemaphoreType.DMA(()),
            pltpu.SemaphoreType.DMA((2, 6)),
            pltpu.SemaphoreType.DMA((2, 6)),
        ],
        compiler_params=pltpu.CompilerParams(collective_id=0, has_side_effects=True),
    )(velocity)


def blend(a, b, c, e, f):
    s1 = 13.0 / 12.0 * (a - 2.0 * b + c) ** 2 + 0.25 * (a - 4.0 * b + 3.0 * c) ** 2
    s2 = 13.0 / 12.0 * (b - 2.0 * c + e) ** 2 + 0.25 * (b - e) ** 2
    s3 = 13.0 / 12.0 * (c - 2.0 * e + f) ** 2 + 0.25 * (3.0 * c - 4.0 * e + f) ** 2
    a1, a2, a3 = [(weno_floor + s) ** 2 for s in (s1, s2, s3)]
    n1, n2, n3 = 0.1 * (a2 * a3), 0.6 * (a1 * a3), 0.3 * (a1 * a2)
    p1 = a * (1.0 / 3.0) - b * (7.0 / 6.0) + c * (11.0 / 6.0)
    p2 = b * (-1.0 / 6.0) + c * (5.0 / 6.0) + e * (1.0 / 3.0)
    p3 = c * (1.0 / 3.0) + e * (5.0 / 6.0) - f * (1.0 / 6.0)
    return (n1 * p1 + n2 * p2 + n3 * p3) / (n1 + n2 + n3)


def bubble_kernel(
    corners, owners, v_ref, lev_ref, step_ref, o_ref, set_ref, ben_ref,
    lev, mot, psa, psb, gain, force, part, nrm, native_a, native_b,
):
    edge = lev.shape[0]
    rows, lanes = lev.shape[1:]
    groups = rows // edge
    per = lanes // edge
    halves = edge // 8
    row, lane = iota((rows, lanes), 0), iota((rows, lanes), 1)
    j_at, k_at = row % edge, lane % edge
    j_first, j_last = j_at == 0, j_at == edge - 1
    k_first, k_last = k_at == 0, k_at == edge - 1

    def prev_j(x):
        return jnp.where(j_first, x, pltpu.roll(x, 1, 0))

    def next_j(x):
        return jnp.where(j_last, x, pltpu.roll(x, rows - 1, 0))

    def prev_k(x):
        return jnp.where(k_first, x, pltpu.roll(x, 1, 1))

    def next_k(x):
        return jnp.where(k_last, x, pltpu.roll(x, lanes - 1, 1))

    def swap_blocks(x):
        block = lane // edge
        for b in (1, 2, 4):
            low = jnp.logical_and((row & b) != 0, (block & b) == 0)
            high = jnp.logical_and((row & b) == 0, (block & b) != 0)
            down = pltpu.roll(pltpu.roll(x, b, 0), lanes - edge * b, 1)
            up = pltpu.roll(pltpu.roll(x, rows - b, 0), edge * b, 1)
            x = jnp.where(low, down, jnp.where(high, up, x))
        return x

    for h in range(halves):
        native_a[h] = lev_ref[:, pl.ds(h * lanes, lanes)]

    def fetch(i, carry):
        pieces = [
            native_a[h, pl.ds(g * per * edge + i, per, stride=edge), :]
            for g in range(groups)
            for h in range(halves)
        ]
        lev[i] = swap_blocks(jnp.concatenate(pieces, axis=0))
        return carry

    lax.fori_loop(0, edge, fetch, 0)

    def write(ref, i, value):
        value = swap_blocks(value)
        for g in range(groups):
            for h in range(halves):
                at = g * edge + h * 8
                ref[h, pl.ds(g * per * edge + i, per, stride=edge), :] = value[at : at + 8]

    slot_lane = iota((edge, lanes), 1) // edge
    for g in range(groups):
        places = [[corners[g * per + s, d] for d in range(3)] for s in range(per)]
        turns = [lax.rem(s * edge + lanes - places[s][2], lanes) for s in range(per)]

        def gather(i, carry, g=g, places=places, turns=turns):
            for c in range(3):
                acc = jnp.zeros((edge, lanes), jnp.float32)
                for s in range(per):
                    block = v_ref[c, places[s][0] + i, pl.ds(places[s][1], edge), :]
                    acc = jnp.where(slot_lane == s, pltpu.roll(block, turns[s], 1), acc)
                mot[c, i, pl.ds(g * edge, edge), :] = acc
            return carry

        lax.fori_loop(0, edge, gather, 0)

    def advect(i, carry):
        here = lev[i]
        change = jnp.zeros_like(here)
        for d in range(3):
            if d == 0:
                slopes = []
                for t in range(-2, 4):
                    at = jnp.clip(i + t, 0, edge - 1)
                    slopes.append(lev[at] - lev[jnp.maximum(at - 1, 0)])
            else:
                back, ahead = (prev_j, next_j) if d == 1 else (prev_k, next_k)
                mid = here - back(here)
                b1 = back(mid)
                f1 = ahead(mid)
                f2 = ahead(f1)
                slopes = [back(b1), b1, mid, f1, f2, ahead(f2)]
            speed = mot[d, i]
            pos = speed > 0.0
            picks = [jnp.where(pos, slopes[n], slopes[5 - n]) for n in range(5)]
            change = change + speed * blend(*picks)
        out = here - box_step * change
        psa[i] = out
        gain[i] = pseudo_step * out * lax.rsqrt(out * out + 1.0)
        return carry

    lax.fori_loop(0, edge, advect, 0)

    def sweep(src, dst):
        for i in range(edge):
            cur = src[i]
            rate = gain[i]
            sign = jnp.where(rate > 0.0, 1.0, -1.0)
            signed = sign * cur
            total = None
            for lo, hi in (
                (src[max(i - 1, 0)], src[min(i + 1, edge - 1)]),
                (prev_j(cur), next_j(cur)),
                (prev_k(cur), next_k(cur)),
            ):
                rise = jnp.maximum(signed - jnp.minimum(sign * lo, sign * hi), 0.0)
                total = rise * rise if total is None else total + rise * rise
            root = total * lax.rsqrt(jnp.maximum(total, tiny))
            dst[i] = cur - rate * (root - 1.0)

    def two_sweeps(n, carry):
        sweep(psa, psb)
        sweep(psb, psa)
        return carry

    lax.fori_loop(0, ITERS // 2, two_sweeps, 0)

    alive = jnp.zeros((rows, lanes), jnp.float32)
    owner_at = (row // edge) * per + lane // edge
    for s in range(groups * per):
        alive = jnp.where(owner_at == s, jnp.where(owners[s] >= 0, 1.0, 0.0), alive)

    def bend(i, carry):
        cur = psa[i]
        c0 = 0.5 * (psa[jnp.minimum(i + 1, edge - 1)] - psa[jnp.maximum(i - 1, 0)])
        c1 = 0.5 * (next_j(cur) - prev_j(cur))
        c2 = 0.5 * (next_k(cur) - prev_k(cur))
        inverse = lax.rsqrt(jnp.maximum(c0 * c0 + c1 * c1 + c2 * c2, normal_floor * normal_floor))
        n1, n2 = c1 * inverse, c2 * inverse
        nrm[i] = c0 * inverse
        part[i] = 0.5 * (next_j(n1) - prev_j(n1)) + 0.5 * (next_k(n2) - prev_k(n2))
        force[0, i] = c0
        force[1, i] = c1
        force[2, i] = c2
        return carry

    lax.fori_loop(0, edge, bend, 0)

    def push(i, carry):
        level = psa[i] * alive
        curve = (
            part[i] + 0.5 * (nrm[jnp.minimum(i + 1, edge - 1)] - nrm[jnp.maximum(i - 1, 0)])
        ) * alive
        write(native_a, i, level)
        write(native_b, i, curve)
        ratio = level * (1.0 / band_width)
        scale = grid_step * tension / (band_width * math.sqrt(math.pi))
        strength = scale * curve * jnp.exp(-(ratio * ratio)) * alive
        for d in range(3):
            force[d, i] = force[d, i] * strength
        return carry

    lax.fori_loop(0, edge, push, 0)
    for h in range(halves):
        set_ref[:, pl.ds(h * lanes, lanes)] = native_a[h]
        ben_ref[:, pl.ds(h * lanes, lanes)] = native_b[h]

    o_ref[...] = step_ref[...]
    wide = iota((edge, lanes), 1)
    for g in range(groups):
        for s in range(per):
            n = g * per + s
            ax, ay, az = corners[n, 0], corners[n, 1], corners[n, 2]
            turn = lax.rem(az + lanes - s * edge, lanes)
            inside = jnp.logical_and(wide >= az, wide < az + edge)

            def deposit(i, carry, g=g, ax=ax, ay=ay, turn=turn, inside=inside):
                for c in range(3):
                    block = pltpu.roll(force[c, i, pl.ds(g * edge, edge), :], turn, 1)
                    at = (c, ax + i, pl.ds(ay, edge), slice(None))
                    o_ref[at] = o_ref[at] + jnp.where(inside, block, 0.0)
                return carry

            lax.fori_loop(0, edge, deposit, 0, unroll=2)


def bubbles(velocity, box_level, corners, owner_list, stepped):
    slots, edge, plane = box_level.shape
    lanes = velocity.shape[3]
    rows = slots * edge * plane // (edge * lanes)
    flat = (slots * edge, plane)
    f32 = jnp.float32
    whole = pl.BlockSpec(memory_space=pltpu.VMEM)
    smem = pl.BlockSpec(memory_space=pltpu.SMEM)
    field = pltpu.VMEM((edge, rows, lanes), f32)
    triple = pltpu.VMEM((3, edge, rows, lanes), f32)
    native = pltpu.VMEM((plane // lanes, slots * edge, lanes), f32)
    result, settled, bending = pl.pallas_call(
        bubble_kernel,
        out_shape=(
            jax.ShapeDtypeStruct(velocity.shape, f32),
            jax.ShapeDtypeStruct(flat, f32),
            jax.ShapeDtypeStruct(flat, f32),
        ),
        in_specs=[smem, smem, whole, whole, whole],
        out_specs=(whole, whole, whole),
        scratch_shapes=[field, triple, field, field, field, triple, field, field, native, native],
    )(corners, owner_list, velocity, box_level.reshape(flat), stepped)
    return result, settled.reshape(box_level.shape), bending.reshape(box_level.shape)


def local(velocity, box_level, corners, owner_list):
    stepped = momentum(velocity)
    return bubbles(velocity, box_level, corners, owner_list, stepped)


def solution(mesh):
    placed = (
        P(None, "gx", "gy", "gz"),
        P(("gx", "gy", "gz"), None, None),
        P(("gx", "gy", "gz"), None),
        P(("gx", "gy", "gz")),
    )
    return jax.shard_map(
        local,
        mesh=mesh,
        in_specs=placed,
        out_specs=(
            P(None, "gx", "gy", "gz"),
            P(("gx", "gy", "gz"), None, None),
            P(("gx", "gy", "gz"), None, None),
        ),
        check_vma=False,
    )
```

```python
import functools
import math

import jax
import jax.numpy as jnp
from jax import lax
from jax.experimental import pallas as pl
from jax.experimental.pallas import tpu as pltpu
from jax.sharding import PartitionSpec as P

ITERS = 12

box_step = 0.25
pseudo_step = 0.3
weno_floor = 1e-06
band_width = 1.5
tension = 2.0
grid_step = 0.2
viscosity = 0.1
normal_floor = 0.5
tiny = 1.1754944e-38

FETCH, GATHER, ADVECT, SECTION, BEND, PUSH, DEPOSIT = 4, 1, 2, 2, 4, 2, 4

MESH = pl.DeviceIdType.MESH


def iota(shape, dim):
    return lax.broadcasted_iota(jnp.int32, shape, dim)


def blend(a, b, c, e, f):
    s1 = 13.0 / 12.0 * (a - 2.0 * b + c) ** 2 + 0.25 * (a - 4.0 * b + 3.0 * c) ** 2
    s2 = 13.0 / 12.0 * (b - 2.0 * c + e) ** 2 + 0.25 * (b - e) ** 2
    s3 = 13.0 / 12.0 * (c - 2.0 * e + f) ** 2 + 0.25 * (3.0 * c - 4.0 * e + f) ** 2
    a1, a2, a3 = [(weno_floor + s) ** 2 for s in (s1, s2, s3)]
    n1, n2, n3 = 0.1 * (a2 * a3), 0.6 * (a1 * a3), 0.3 * (a1 * a2)
    p1 = a * (1.0 / 3.0) - b * (7.0 / 6.0) + c * (11.0 / 6.0)
    p2 = b * (-1.0 / 6.0) + c * (5.0 / 6.0) + e * (1.0 / 3.0)
    p3 = c * (1.0 / 3.0) + e * (5.0 / 6.0) - f * (1.0 / 6.0)
    return (n1 * p1 + n2 * p2 + n3 * p3) / (n1 + n2 + n3)


class Box:
    def __init__(self, edge, rows, lanes):
        self.edge, self.rows, self.lanes = edge, rows, lanes
        self.row, self.lane = iota((rows, lanes), 0), iota((rows, lanes), 1)
        j_at, k_at = self.row % edge, self.lane % edge
        self.j_first, self.j_last = j_at == 0, j_at == edge - 1
        self.k_first, self.k_last = k_at == 0, k_at == edge - 1
        self.groups = rows // edge
        self.per = lanes // edge
        self.halves = edge // 8

    def prev_j(self, x):
        return jnp.where(self.j_first, x, pltpu.roll(x, 1, 0))

    def next_j(self, x):
        return jnp.where(self.j_last, x, pltpu.roll(x, self.rows - 1, 0))

    def prev_k(self, x):
        return jnp.where(self.k_first, x, pltpu.roll(x, 1, 1))

    def next_k(self, x):
        return jnp.where(self.k_last, x, pltpu.roll(x, self.lanes - 1, 1))

    def swap_blocks(self, x):
        block = self.lane // self.edge
        for b in (1, 2, 4):
            low = jnp.logical_and((self.row & b) != 0, (block & b) == 0)
            high = jnp.logical_and((self.row & b) == 0, (block & b) != 0)
            down = pltpu.roll(pltpu.roll(x, b, 0), self.lanes - self.edge * b, 1)
            up = pltpu.roll(pltpu.roll(x, self.rows - b, 0), self.edge * b, 1)
            x = jnp.where(low, down, jnp.where(high, up, x))
        return x


def fetch_levels(box, lev_ref, native, lev):
    edge, per, lanes = box.edge, box.per, box.lanes
    for h in range(box.halves):
        native[h] = lev_ref[:, pl.ds(h * lanes, lanes)]

    def fetch(i, carry):
        pieces = [
            native[h, pl.ds(g * per * edge + i, per, stride=edge), :]
            for g in range(box.groups)
            for h in range(box.halves)
        ]
        lev[i] = box.swap_blocks(jnp.concatenate(pieces, axis=0))
        return carry

    lax.fori_loop(0, edge, fetch, 0, unroll=FETCH)


def gather_motion(box, corners, v_ref, mot):
    edge, per, lanes = box.edge, box.per, box.lanes
    slot_lane = iota((edge, lanes), 1) // edge
    for g in range(box.groups):
        places = [[corners[d, g * per + s] for d in range(3)] for s in range(per)]
        turns = [lax.rem(s * edge + lanes - places[s][2], lanes) for s in range(per)]

        def gather(i, carry, g=g, places=places, turns=turns):
            for c in range(3):
                acc = jnp.zeros((edge, lanes), jnp.float32)
                for s in range(per):
                    block = v_ref[c, places[s][0] + i, pl.ds(places[s][1], edge), :]
                    acc = jnp.where(slot_lane == s, pltpu.roll(block, turns[s], 1), acc)
                mot[c, i, pl.ds(g * edge, edge), :] = acc
            return carry

        lax.fori_loop(0, edge, gather, 0, unroll=GATHER)


def advect_levels(box, lev, slope, mot, psa, gain):
    edge = box.edge

    def rise(i, carry):
        slope[i + 3] = lev[i + 1] - lev[i]
        return carry

    zero = jnp.zeros_like(lev[0])
    for n in range(3):
        slope[n] = zero
    lax.fori_loop(0, edge - 1, rise, 0, unroll=5)
    for n in range(3):
        slope[edge + 2 + n] = slope[edge + 1]

    def advect(i, carry):
        here = lev[i]
        change = jnp.zeros_like(here)
        for d in range(3):
            if d == 0:
                slopes = [slope[i + n] for n in range(6)]
            else:
                back, ahead = (box.prev_j, box.next_j) if d == 1 else (box.prev_k, box.next_k)
                mid = here - back(here)
                b1 = back(mid)
                f1 = ahead(mid)
                f2 = ahead(f1)
                slopes = [back(b1), b1, mid, f1, f2, ahead(f2)]
            speed = mot[d, i]
            pos = speed > 0.0
            picks = [jnp.where(pos, slopes[n], slopes[5 - n]) for n in range(5)]
            change = change + speed * blend(*picks)
        out = here - box_step * change
        psa[i] = out
        gain[i] = pseudo_step * out * lax.rsqrt(out * out + 1.0)
        return carry

    lax.fori_loop(0, edge, advect, 0, unroll=ADVECT)


def reinitialize(box, psa, psb, gain):
    edge = box.edge

    def sweep(src, dst):
        for i in range(edge):
            cur = src[i]
            rate = gain[i]
            sign = jnp.where(rate > 0.0, 1.0, -1.0)
            signed = sign * cur
            total = None
            for lo, hi in (
                (src[max(i - 1, 0)], src[min(i + 1, edge - 1)]),
                (box.prev_j(cur), box.next_j(cur)),
                (box.prev_k(cur), box.next_k(cur)),
            ):
                rise = jnp.maximum(signed - jnp.minimum(sign * lo, sign * hi), 0.0)
                total = rise * rise if total is None else total + rise * rise
            root = total * lax.rsqrt(jnp.maximum(total, tiny))
            dst[i] = cur - rate * (root - 1.0)

    def two_sweeps(n, carry):
        sweep(psa, psb)
        sweep(psb, psa)
        return carry

    lax.fori_loop(0, ITERS // 2, two_sweeps, 0)


def pack_z(src, dst, xs, ys, lanes):
    group = iota((ys, lanes), 1) // 4

    def step(x, accs):
        shift = 4 * x + 1
        return tuple(
            jnp.where(group == x, pltpu.roll(src[c, x], shift, 1), accs[c]) for c in range(3)
        )

    accs = lax.fori_loop(
        0, xs, step, tuple(jnp.zeros((ys, lanes), jnp.float32) for _ in range(3)), unroll=8
    )
    for c in range(3):
        dst[c] = accs[c]


def step_kernel(
    sizes, corners, v_hbm, lev_ref, o_ref, psi_ref,
    vel, pred, xrecv, ysend, yrecv, zsend, zrecv, comb, lev, slope, mot, psb, gain, native,
    local_sem, send_sem, recv_sem,
):
    _, xs, ys, lanes = v_hbm.shape
    box = Box(*lev.shape)
    load = pltpu.make_async_copy(v_hbm, vel, local_sem)
    load.start()
    ups, downs = [], []
    for axis in ("gx", "gy", "gz"):
        me, n = lax.axis_index(axis), sizes[axis]
        ups.append({axis: lax.rem(me + 1, n)})
        downs.append({axis: lax.rem(me + n - 1, n)})
    barrier = pltpu.get_barrier_semaphore()
    for target in ups + downs:
        pl.semaphore_signal(barrier, inc=1, device_id=target, device_id_type=MESH)
    fetch_levels(box, lev_ref, native, lev)
    load.wait()

    def pack(r, src):
        for c in range(3):
            ysend[r, 0, c] = src[c, :, ys - 1, :]
            ysend[r, 1, c] = src[c, :, 0, :]
        pack_z(src, zsend.at[r], xs, ys, lanes)

    def exchange(r, src):
        copies = []

        def send(n, src, dst, target):
            copy = pltpu.make_async_remote_copy(
                src_ref=src,
                dst_ref=dst,
                send_sem=send_sem.at[r, n],
                recv_sem=recv_sem.at[r, n],
                device_id=target,
                device_id_type=MESH,
            )
            copy.start()
            copies.append(copy)

        send(0, src.at[:, xs - 1], xrecv.at[r, 0], ups[0])
        send(1, src.at[:, 0], xrecv.at[r, 1], downs[0])
        send(2, ysend.at[r, 0], yrecv.at[r, 0], ups[1])
        send(3, ysend.at[r, 1], yrecv.at[r, 1], downs[1])
        send(4, zsend.at[r], zrecv.at[r, 0], ups[2])
        send(5, zsend.at[r], zrecv.at[r, 1], downs[2])
        return copies

    lane = iota((ys, lanes), 1)
    row = iota((ys, lanes), 0)
    quarter = lane % 4

    def section(r, src, emit):
        for c in range(3):
            comb[c] = jnp.where(
                quarter == 0,
                pltpu.roll(zrecv[r, 1, c], lanes - 1, 1),
                pltpu.roll(zrecv[r, 0, c], 1, 1),
            )

        def plane(x, before, after):
            centre = [src[c, x] for c in range(3)]
            for c in range(3):
                mid = centre[c]
                x_lo, x_hi = before(c), after(c)
                y_lo = jnp.where(row == 0, yrecv[r, 0, c, pl.ds(x, 1), :], pltpu.roll(mid, 1, 0))
                y_hi = jnp.where(
                    row == ys - 1, yrecv[r, 1, c, pl.ds(x, 1), :], pltpu.roll(mid, ys - 1, 0)
                )
                halo = pltpu.roll(comb[c], lanes - 1 - 4 * x, 1)
                z_lo = jnp.where(lane == 0, halo, pltpu.roll(mid, 1, 1))
                z_hi = jnp.where(lane == lanes - 1, halo, pltpu.roll(mid, lanes - 1, 1))
                spread = (x_hi + x_lo) + (y_hi + y_lo) + (z_hi + z_lo) - 6.0 * mid
                advect = (
                    centre[0] * (x_hi - x_lo) + centre[1] * (y_hi - y_lo) + centre[2] * (z_hi - z_lo)
                )
                emit(c, x, mid + grid_step * (viscosity * spread - 0.5 * advect))

        def step(x, carry):
            plane(x, lambda c: src[c, x - 1], lambda c: src[c, x + 1])
            return carry

        plane(0, lambda c: xrecv[r, 0, c], lambda c: src[c, 1])
        lax.fori_loop(1, xs - 1, step, 0, unroll=SECTION)
        plane(xs - 1, lambda c: src[c, xs - 2], lambda c: xrecv[r, 1, c])

    def first(c, x, value):
        pred[c, x] = value

    def second(c, x, value):
        o_ref[c, x] = 0.5 * (vel[c, x] + value)

    pack(0, vel)
    pl.semaphore_wait(barrier, 6)
    copies = exchange(0, vel)
    gather_motion(box, corners, vel, mot)
    advect_levels(box, lev, slope, mot, psi_ref, gain)
    for copy in copies:
        copy.wait()
    section(0, vel, first)
    pack(1, pred)
    copies = exchange(1, pred)
    reinitialize(box, psi_ref, psb, gain)
    for copy in copies:
        copy.wait()
    section(1, pred, second)


def step_call(velocity, box_level, corners):
    sizes = {axis: lax.axis_size(axis) for axis in ("gx", "gy", "gz")}
    _, xs, ys, lanes = velocity.shape
    slots, edge, plane = box_level.shape
    rows = slots * edge * plane // (edge * lanes)
    vmem = pltpu.VMEM
    f32 = jnp.float32
    whole = pl.BlockSpec(memory_space=pltpu.VMEM)
    return pl.pallas_call(
        functools.partial(step_kernel, sizes),
        out_shape=(
            jax.ShapeDtypeStruct(velocity.shape, f32),
            jax.ShapeDtypeStruct((edge, rows, lanes), f32),
        ),
        in_specs=[
            pl.BlockSpec(memory_space=pltpu.SMEM),
            pl.BlockSpec(memory_space=pl.ANY),
            whole,
        ],
        out_specs=(whole, whole),
        scratch_shapes=[
            vmem(velocity.shape, f32),
            vmem(velocity.shape, f32),
            vmem((2, 2, 3, ys, lanes), f32),
            vmem((2, 2, 3, xs, lanes), f32),
            vmem((2, 2, 3, xs, lanes), f32),
            vmem((2, 3, ys, lanes), f32),
            vmem((2, 2, 3, ys, lanes), f32),
            vmem((3, ys, lanes), f32),
            vmem((edge, rows, lanes), f32),
            vmem((edge + 5, rows, lanes), f32),
            vmem((3, edge, rows, lanes), f32),
            vmem((edge, rows, lanes), f32),
            vmem((edge, rows, lanes), f32),
            vmem((plane // lanes, slots * edge, lanes), f32),
            pltpu.SemaphoreType.DMA(()),
            pltpu.SemaphoreType.DMA((2, 6)),
            pltpu.SemaphoreType.DMA((2, 6)),
        ],
        compiler_params=pltpu.CompilerParams(collective_id=0, has_side_effects=True),
    )(corners, velocity, box_level.reshape(slots * edge, plane))


def force_kernel(
    corners, owners, psi, step_hbm, o_ref, set_ref, ben_ref, force, part, nrm, native_a, native_b, sem
):
    load = pltpu.make_async_copy(step_hbm, o_ref, sem)
    load.start()
    box = Box(*psi.shape)
    edge, per, groups, lanes = box.edge, box.per, box.groups, box.lanes

    def write(ref, i, value):
        value = box.swap_blocks(value)
        for g in range(groups):
            for h in range(box.halves):
                at = g * edge + h * 8
                ref[h, pl.ds(g * per * edge + i, per, stride=edge), :] = value[at : at + 8]

    alive = jnp.zeros((box.rows, lanes), jnp.float32)
    owner_at = (box.row // edge) * per + box.lane // edge
    for s in range(groups * per):
        alive = jnp.where(owner_at == s, jnp.where(owners[s] >= 0, 1.0, 0.0), alive)

    def bend(i, carry):
        cur = psi[i]
        c0 = 0.5 * (psi[jnp.minimum(i + 1, edge - 1)] - psi[jnp.maximum(i - 1, 0)])
        c1 = 0.5 * (box.next_j(cur) - box.prev_j(cur))
        c2 = 0.5 * (box.next_k(cur) - box.prev_k(cur))
        inverse = lax.rsqrt(jnp.maximum(c0 * c0 + c1 * c1 + c2 * c2, normal_floor * normal_floor))
        n1, n2 = c1 * inverse, c2 * inverse
        nrm[i] = c0 * inverse
        part[i] = 0.5 * (box.next_j(n1) - box.prev_j(n1)) + 0.5 * (box.next_k(n2) - box.prev_k(n2))
        force[0, i] = c0
        force[1, i] = c1
        force[2, i] = c2
        return carry

    lax.fori_loop(0, edge, bend, 0, unroll=BEND)

    def push(i, carry):
        level = psi[i] * alive
        curve = (
            part[i] + 0.5 * (nrm[jnp.minimum(i + 1, edge - 1)] - nrm[jnp.maximum(i - 1, 0)])
        ) * alive
        write(native_a, i, level)
        write(native_b, i, curve)
        ratio = level * (1.0 / band_width)
        scale = grid_step * tension / (band_width * math.sqrt(math.pi))
        strength = scale * curve * jnp.exp(-(ratio * ratio)) * alive
        for d in range(3):
            force[d, i] = force[d, i] * strength
        return carry

    lax.fori_loop(0, edge, push, 0, unroll=PUSH)
    for h in range(box.halves):
        set_ref[:, pl.ds(h * lanes, lanes)] = native_a[h]
        ben_ref[:, pl.ds(h * lanes, lanes)] = native_b[h]

    load.wait()
    wide = iota((edge, lanes), 1)

    def deposit_slot(n, carry):
        g, s = n // per, n % per
        ax, ay, az = corners[0, n], corners[1, n], corners[2, n]
        turn = lax.rem(az + lanes - s * edge, lanes)
        inside = jnp.logical_and(wide >= az, wide < az + edge)
        first_row = pl.multiple_of(g * edge, edge)

        for i in range(0, edge, DEPOSIT):
            spots = [(c, i + t) for t in range(DEPOSIT) for c in range(3)]
            blocks = [pltpu.roll(force[c, q, pl.ds(first_row, edge), :], turn, 1) for c, q in spots]
            olds = [o_ref[c, ax + q, pl.ds(ay, edge), :] for c, q in spots]
            news = [old + jnp.where(inside, block, 0.0) for old, block in zip(olds, blocks)]
            for (c, q), new in zip(spots, news):
                o_ref[c, ax + q, pl.ds(ay, edge), :] = new
        return carry

    lax.fori_loop(0, groups * per, deposit_slot, 0)


def force_call(shapes, psi, corners, owner_list, stepped):
    slots, edge, plane = shapes
    rows, lanes = psi.shape[1:]
    flat = (slots * edge, plane)
    f32 = jnp.float32
    whole = pl.BlockSpec(memory_space=pltpu.VMEM)
    smem = pl.BlockSpec(memory_space=pltpu.SMEM)
    field = pltpu.VMEM((edge, rows, lanes), f32)
    native = pltpu.VMEM((plane // lanes, slots * edge, lanes), f32)
    result, settled, bending = pl.pallas_call(
        force_kernel,
        out_shape=(
            jax.ShapeDtypeStruct(stepped.shape, f32),
            jax.ShapeDtypeStruct(flat, f32),
            jax.ShapeDtypeStruct(flat, f32),
        ),
        in_specs=[smem, smem, whole, pl.BlockSpec(memory_space=pl.ANY)],
        out_specs=(whole, whole, whole),
        scratch_shapes=[
            pltpu.VMEM((3, edge, rows, lanes), f32),
            field,
            field,
            native,
            native,
            pltpu.SemaphoreType.DMA(()),
        ],
    )(corners, owner_list, psi, stepped)
    return result, settled.reshape(shapes), bending.reshape(shapes)


def local(velocity, box_level, corners, owner_list):
    turned = corners.T
    stepped, psi = step_call(velocity, box_level, turned)
    return force_call(box_level.shape, psi, turned, owner_list, stepped)


def solution(mesh):
    placed = (
        P(None, "gx", "gy", "gz"),
        P(("gx", "gy", "gz"), None, None),
        P(("gx", "gy", "gz"), None),
        P(("gx", "gy", "gz")),
    )
    return jax.shard_map(
        local,
        mesh=mesh,
        in_specs=placed,
        out_specs=(
            P(None, "gx", "gy", "gz"),
            P(("gx", "gy", "gz"), None, None),
            P(("gx", "gy", "gz"), None, None),
        ),
        check_vma=False,
    )
```

```python
import functools
import math

import jax
import jax.numpy as jnp
from jax import lax
from jax.experimental import pallas as pl
from jax.experimental.pallas import tpu as pltpu
from jax.sharding import PartitionSpec as P

ITERS = 12

box_step = 0.25
pseudo_step = 0.3
weno_floor = 1e-06
band_width = 1.5
tension = 2.0
grid_step = 0.2
viscosity = 0.1
normal_floor = 0.5
tiny = 1.1754944e-38

FETCH, GATHER, ADVECT, SECTION, BEND, PUSH, DEPOSIT = 4, 2, 4, 5, 4, 4, 4

MESH = pl.DeviceIdType.MESH


def iota(shape, dim):
    return lax.broadcasted_iota(jnp.int32, shape, dim)


def blend(a, b, c, e, f):
    d1, d2, d3, d4 = a - b, b - c, c - e, e - f
    twice, thrice = 3.0 * d2, 3.0 * d3
    x1, x2, x3 = d1 - d2, d2 - d3, d3 - d4
    y1, y2, y3 = d1 - twice, d2 + d3, thrice - d4
    a1, a2, a3 = [
        (4.0 * weno_floor + (y * y + 13.0 / 3.0 * (x * x))) ** 2
        for x, y in ((x1, y1), (x2, y2), (x3, y3))
    ]
    n1, n2, n3 = a2 * a3, a1 * (6.0 * a3), a1 * (3.0 * a2)
    q1 = 2.0 * d1 - 5.0 * d2
    q2 = d2 + 2.0 * d3
    q3 = d4 - 4.0 * d3
    return c + (n1 * q1 - n2 * q2 + n3 * q3) / (6.0 * (n1 + n2 + n3))


class Box:
    def __init__(self, edge, rows, lanes):
        self.edge, self.rows, self.lanes = edge, rows, lanes
        self.row, self.lane = iota((rows, lanes), 0), iota((rows, lanes), 1)
        j_at, k_at = self.row % edge, self.lane % edge
        self.j_first, self.j_last = j_at == 0, j_at == edge - 1
        self.k_first, self.k_last = k_at == 0, k_at == edge - 1
        self.groups = rows // edge
        self.per = lanes // edge
        self.halves = edge // 8

    def prev_j(self, x):
        return jnp.where(self.j_first, x, pltpu.roll(x, 1, 0))

    def next_j(self, x):
        return jnp.where(self.j_last, x, pltpu.roll(x, self.rows - 1, 0))

    def prev_k(self, x):
        return jnp.where(self.k_first, x, pltpu.roll(x, 1, 1))

    def next_k(self, x):
        return jnp.where(self.k_last, x, pltpu.roll(x, self.lanes - 1, 1))

    def swap_blocks(self, x):
        block = self.lane // self.edge
        for b in (1, 2, 4):
            low = jnp.logical_and((self.row & b) != 0, (block & b) == 0)
            high = jnp.logical_and((self.row & b) == 0, (block & b) != 0)
            down = pltpu.roll(pltpu.roll(x, b, 0), self.lanes - self.edge * b, 1)
            up = pltpu.roll(pltpu.roll(x, self.rows - b, 0), self.edge * b, 1)
            x = jnp.where(low, down, jnp.where(high, up, x))
        return x


def fetch_levels(box, lev_ref, native, lev):
    edge, per, lanes = box.edge, box.per, box.lanes
    for h in range(box.halves):
        native[h] = lev_ref[:, pl.ds(h * lanes, lanes)]

    def fetch(i, carry):
        pieces = [
            native[h, pl.ds(g * per * edge + i, per, stride=edge), :]
            for g in range(box.groups)
            for h in range(box.halves)
        ]
        lev[i] = box.swap_blocks(jnp.concatenate(pieces, axis=0))
        return carry

    lax.fori_loop(0, edge, fetch, 0, unroll=FETCH)


def gather_motion(box, corners, v_ref, mot):
    edge, per, lanes = box.edge, box.per, box.lanes
    slot_lane = iota((edge, lanes), 1) // edge
    for g in range(box.groups):
        places = [[corners[d, g * per + s] for d in range(3)] for s in range(per)]
        turns = [lax.rem(s * edge + lanes - places[s][2], lanes) for s in range(per)]

        def gather(i, carry, g=g, places=places, turns=turns):
            for c in range(3):
                acc = jnp.zeros((edge, lanes), jnp.float32)
                for s in range(per):
                    block = v_ref[c, places[s][0] + i, pl.ds(places[s][1], edge), :]
                    acc = jnp.where(slot_lane == s, pltpu.roll(block, turns[s], 1), acc)
                mot[c, i, pl.ds(g * edge, edge), :] = acc
            return carry

        lax.fori_loop(0, edge, gather, 0, unroll=GATHER)


def advect_levels(box, lev, slope, mot, psa, gain):
    edge = box.edge

    def rise(i, carry):
        slope[i + 3] = lev[i + 1] - lev[i]
        return carry

    zero = jnp.zeros_like(lev[0])
    for n in range(3):
        slope[n] = zero
    lax.fori_loop(0, edge - 1, rise, 0, unroll=5)
    for n in range(3):
        slope[edge + 2 + n] = slope[edge + 1]

    def advect(i, carry):
        here = lev[i]
        change = jnp.zeros_like(here)
        for d in range(3):
            if d == 0:
                slopes = [slope[i + n] for n in range(6)]
            else:
                back, ahead = (box.prev_j, box.next_j) if d == 1 else (box.prev_k, box.next_k)
                mid = here - back(here)
                b1 = back(mid)
                f1 = ahead(mid)
                f2 = ahead(f1)
                slopes = [back(b1), b1, mid, f1, f2, ahead(f2)]
            speed = mot[d, i]
            pos = speed > 0.0
            picks = [jnp.where(pos, slopes[n], slopes[5 - n]) for n in range(5)]
            change = change + speed * blend(*picks)
        out = here - box_step * change
        psa[i] = out
        gain[i] = pseudo_step * out * lax.rsqrt(out * out + 1.0)
        return carry

    lax.fori_loop(0, edge, advect, 0, unroll=ADVECT)


def reinitialize(box, psa, psb, gain):
    edge = box.edge

    def sweep(src, dst):
        for i in range(edge):
            cur = src[i]
            rate = gain[i]
            sign = jnp.where(rate > 0.0, 1.0, -1.0)
            signed = sign * cur
            total = None
            for lo, hi in (
                (src[max(i - 1, 0)], src[min(i + 1, edge - 1)]),
                (box.prev_j(cur), box.next_j(cur)),
                (box.prev_k(cur), box.next_k(cur)),
            ):
                rise = jnp.maximum(signed - jnp.minimum(sign * lo, sign * hi), 0.0)
                total = rise * rise if total is None else total + rise * rise
            root = total * lax.rsqrt(jnp.maximum(total, tiny))
            dst[i] = cur - rate * (root - 1.0)

    def two_sweeps(n, carry):
        sweep(psa, psb)
        sweep(psb, psa)
        return carry

    lax.fori_loop(0, ITERS // 2, two_sweeps, 0)


def pack_z(src, dst, xs, ys, lanes):
    group = iota((ys, lanes), 1) // 4

    def step(x, accs):
        shift = 4 * x + 1
        return tuple(
            jnp.where(group == x, pltpu.roll(src[c, x], shift, 1), accs[c]) for c in range(3)
        )

    accs = lax.fori_loop(
        0, xs, step, tuple(jnp.zeros((ys, lanes), jnp.float32) for _ in range(3)), unroll=8
    )
    for c in range(3):
        dst[c] = accs[c]


def step_kernel(
    sizes, corners, v_hbm, lev_ref, o_hbm, psi_ref,
    vel, out, pred, xrecv, ysend, yrecv, zsend, zrecv, comb, lev, slope, mot, psb, gain, native,
    local_sem, out_sem, send_sem, recv_sem,
):
    _, xs, ys, lanes = v_hbm.shape
    box = Box(*lev.shape)
    load = pltpu.make_async_copy(v_hbm, vel, local_sem)
    load.start()
    ups, downs = [], []
    for axis in ("gx", "gy", "gz"):
        me, n = lax.axis_index(axis), sizes[axis]
        ups.append({axis: lax.rem(me + 1, n)})
        downs.append({axis: lax.rem(me + n - 1, n)})
    barrier = pltpu.get_barrier_semaphore()
    for target in ups + downs:
        pl.semaphore_signal(barrier, inc=1, device_id=target, device_id_type=MESH)
    fetch_levels(box, lev_ref, native, lev)
    load.wait()

    def pack(r, src):
        for c in range(3):
            ysend[r, 0, c] = src[c, :, ys - 1, :]
            ysend[r, 1, c] = src[c, :, 0, :]
        pack_z(src, zsend.at[r], xs, ys, lanes)

    def exchange(r, src):
        copies = []

        def send(n, src, dst, target):
            copy = pltpu.make_async_remote_copy(
                src_ref=src,
                dst_ref=dst,
                send_sem=send_sem.at[r, n],
                recv_sem=recv_sem.at[r, n],
                device_id=target,
                device_id_type=MESH,
            )
            copy.start()
            copies.append(copy)

        send(0, src.at[:, xs - 1], xrecv.at[r, 0], ups[0])
        send(1, src.at[:, 0], xrecv.at[r, 1], downs[0])
        send(2, ysend.at[r, 0], yrecv.at[r, 0], ups[1])
        send(3, ysend.at[r, 1], yrecv.at[r, 1], downs[1])
        send(4, zsend.at[r], zrecv.at[r, 0], ups[2])
        send(5, zsend.at[r], zrecv.at[r, 1], downs[2])
        return copies

    lane = iota((ys, lanes), 1)
    row = iota((ys, lanes), 0)
    quarter = lane % 4

    half = xs // 2

    def store(n):
        part = pl.ds(n * half, half)
        return pltpu.make_async_copy(out.at[:, part], o_hbm.at[:, part], out_sem.at[n])

    def section(r, src, emit, done):
        for c in range(3):
            comb[c] = jnp.where(
                quarter == 0,
                pltpu.roll(zrecv[r, 1, c], lanes - 1, 1),
                pltpu.roll(zrecv[r, 0, c], 1, 1),
            )

        def plane(x, before, after):
            centre = [src[c, x] for c in range(3)]
            for c in range(3):
                mid = centre[c]
                x_lo, x_hi = before(c), after(c)
                y_lo = jnp.where(row == 0, yrecv[r, 0, c, pl.ds(x, 1), :], pltpu.roll(mid, 1, 0))
                y_hi = jnp.where(
                    row == ys - 1, yrecv[r, 1, c, pl.ds(x, 1), :], pltpu.roll(mid, ys - 1, 0)
                )
                halo = pltpu.roll(comb[c], lanes - 1 - 4 * x, 1)
                z_lo = jnp.where(lane == 0, halo, pltpu.roll(mid, 1, 1))
                z_hi = jnp.where(lane == lanes - 1, halo, pltpu.roll(mid, lanes - 1, 1))
                spread = (x_hi + x_lo) + (y_hi + y_lo) + (z_hi + z_lo) - 6.0 * mid
                advect = (
                    centre[0] * (x_hi - x_lo) + centre[1] * (y_hi - y_lo) + centre[2] * (z_hi - z_lo)
                )
                emit(c, x, mid + grid_step * (viscosity * spread - 0.5 * advect))

        def step(x, carry):
            plane(x, lambda c: src[c, x - 1], lambda c: src[c, x + 1])
            return carry

        plane(0, lambda c: xrecv[r, 0, c], lambda c: src[c, 1])
        lax.fori_loop(1, half, step, 0, unroll=SECTION)
        done(0)
        lax.fori_loop(half, xs - 1, step, 0, unroll=SECTION)
        plane(xs - 1, lambda c: src[c, xs - 2], lambda c: xrecv[r, 1, c])
        done(1)

    def first(c, x, value):
        pred[c, x] = value

    def second(c, x, value):
        out[c, x] = 0.5 * (vel[c, x] + value)

    pack(0, vel)
    pl.semaphore_wait(barrier, 6)
    copies = exchange(0, vel)
    gather_motion(box, corners, vel, mot)
    advect_levels(box, lev, slope, mot, psi_ref, gain)
    for copy in copies:
        copy.wait()
    section(0, vel, first, lambda n: None)
    pack(1, pred)
    copies = exchange(1, pred)
    reinitialize(box, psi_ref, psb, gain)
    for copy in copies:
        copy.wait()
    section(1, pred, second, lambda n: store(n).start())
    store(0).wait()
    store(1).wait()


def step_call(velocity, box_level, corners):
    sizes = {axis: lax.axis_size(axis) for axis in ("gx", "gy", "gz")}
    _, xs, ys, lanes = velocity.shape
    slots, edge, plane = box_level.shape
    rows = slots * edge * plane // (edge * lanes)
    vmem = pltpu.VMEM
    f32 = jnp.float32
    whole = pl.BlockSpec(memory_space=pltpu.VMEM)
    return pl.pallas_call(
        functools.partial(step_kernel, sizes),
        out_shape=(
            jax.ShapeDtypeStruct(velocity.shape, f32),
            jax.ShapeDtypeStruct((edge, rows, lanes), f32),
        ),
        in_specs=[
            pl.BlockSpec(memory_space=pltpu.SMEM),
            pl.BlockSpec(memory_space=pl.ANY),
            whole,
        ],
        out_specs=(pl.BlockSpec(memory_space=pl.ANY), whole),
        scratch_shapes=[
            vmem(velocity.shape, f32),
            vmem(velocity.shape, f32),
            vmem(velocity.shape, f32),
            vmem((2, 2, 3, ys, lanes), f32),
            vmem((2, 2, 3, xs, lanes), f32),
            vmem((2, 2, 3, xs, lanes), f32),
            vmem((2, 3, ys, lanes), f32),
            vmem((2, 2, 3, ys, lanes), f32),
            vmem((3, ys, lanes), f32),
            vmem((edge, rows, lanes), f32),
            vmem((edge + 5, rows, lanes), f32),
            vmem((3, edge, rows, lanes), f32),
            vmem((edge, rows, lanes), f32),
            vmem((edge, rows, lanes), f32),
            vmem((plane // lanes, slots * edge, lanes), f32),
            pltpu.SemaphoreType.DMA(()),
            pltpu.SemaphoreType.DMA((2,)),
            pltpu.SemaphoreType.DMA((2, 6)),
            pltpu.SemaphoreType.DMA((2, 6)),
        ],
        compiler_params=pltpu.CompilerParams(collective_id=0, has_side_effects=True),
    )(corners, velocity, box_level.reshape(slots * edge, plane))


def force_kernel(
    corners, owners, psi, step_hbm, o_ref, set_ref, ben_ref, force, part, nrm, native_a, native_b, sem
):
    load = pltpu.make_async_copy(step_hbm, o_ref, sem)
    load.start()
    box = Box(*psi.shape)
    edge, per, groups, lanes = box.edge, box.per, box.groups, box.lanes

    def write(ref, i, value):
        value = box.swap_blocks(value)
        for g in range(groups):
            for h in range(box.halves):
                at = g * edge + h * 8
                ref[h, pl.ds(g * per * edge + i, per, stride=edge), :] = value[at : at + 8]

    alive = jnp.zeros((box.rows, lanes), jnp.float32)
    owner_at = (box.row // edge) * per + box.lane // edge
    for s in range(groups * per):
        alive = jnp.where(owner_at == s, jnp.where(owners[s] >= 0, 1.0, 0.0), alive)

    def bend(i, carry):
        cur = psi[i]
        c0 = 0.5 * (psi[jnp.minimum(i + 1, edge - 1)] - psi[jnp.maximum(i - 1, 0)])
        c1 = 0.5 * (box.next_j(cur) - box.prev_j(cur))
        c2 = 0.5 * (box.next_k(cur) - box.prev_k(cur))
        inverse = lax.rsqrt(jnp.maximum(c0 * c0 + c1 * c1 + c2 * c2, normal_floor * normal_floor))
        n1, n2 = c1 * inverse, c2 * inverse
        nrm[i] = c0 * inverse
        part[i] = 0.5 * (box.next_j(n1) - box.prev_j(n1)) + 0.5 * (box.next_k(n2) - box.prev_k(n2))
        force[0, i] = c0
        force[1, i] = c1
        force[2, i] = c2
        return carry

    lax.fori_loop(0, edge, bend, 0, unroll=BEND)

    def push(i, carry):
        level = psi[i] * alive
        curve = (
            part[i] + 0.5 * (nrm[jnp.minimum(i + 1, edge - 1)] - nrm[jnp.maximum(i - 1, 0)])
        ) * alive
        write(native_a, i, level)
        write(native_b, i, curve)
        ratio = level * (1.0 / band_width)
        scale = grid_step * tension / (band_width * math.sqrt(math.pi))
        strength = scale * curve * jnp.exp(-(ratio * ratio)) * alive
        for d in range(3):
            force[d, i] = force[d, i] * strength
        return carry

    lax.fori_loop(0, edge, push, 0, unroll=PUSH)
    for h in range(box.halves):
        set_ref[:, pl.ds(h * lanes, lanes)] = native_a[h]
        ben_ref[:, pl.ds(h * lanes, lanes)] = native_b[h]

    load.wait()
    wide = iota((edge, lanes), 1)

    def deposit_slot(n, carry):
        g, s = n // per, n % per
        ax, ay, az = corners[0, n], corners[1, n], corners[2, n]
        turn = lax.rem(az + lanes - s * edge, lanes)
        inside = jnp.logical_and(wide >= az, wide < az + edge)
        first_row = pl.multiple_of(g * edge, edge)

        for i in range(0, edge, DEPOSIT):
            spots = [(c, i + t) for t in range(DEPOSIT) for c in range(3)]
            blocks = [pltpu.roll(force[c, q, pl.ds(first_row, edge), :], turn, 1) for c, q in spots]
            olds = [o_ref[c, ax + q, pl.ds(ay, edge), :] for c, q in spots]
            news = [old + jnp.where(inside, block, 0.0) for old, block in zip(olds, blocks)]
            for (c, q), new in zip(spots, news):
                o_ref[c, ax + q, pl.ds(ay, edge), :] = new
        return carry

    lax.fori_loop(0, groups * per, deposit_slot, 0)


def force_call(shapes, psi, corners, owner_list, stepped):
    slots, edge, plane = shapes
    rows, lanes = psi.shape[1:]
    flat = (slots * edge, plane)
    f32 = jnp.float32
    whole = pl.BlockSpec(memory_space=pltpu.VMEM)
    smem = pl.BlockSpec(memory_space=pltpu.SMEM)
    field = pltpu.VMEM((edge, rows, lanes), f32)
    native = pltpu.VMEM((plane // lanes, slots * edge, lanes), f32)
    result, settled, bending = pl.pallas_call(
        force_kernel,
        out_shape=(
            jax.ShapeDtypeStruct(stepped.shape, f32),
            jax.ShapeDtypeStruct(flat, f32),
            jax.ShapeDtypeStruct(flat, f32),
        ),
        in_specs=[smem, smem, whole, pl.BlockSpec(memory_space=pl.ANY)],
        out_specs=(whole, whole, whole),
        scratch_shapes=[
            pltpu.VMEM((3, edge, rows, lanes), f32),
            field,
            field,
            native,
            native,
            pltpu.SemaphoreType.DMA(()),
        ],
    )(corners, owner_list, psi, stepped)
    return result, settled.reshape(shapes), bending.reshape(shapes)


def local(velocity, box_level, corners, owner_list):
    turned = corners.T
    stepped, psi = step_call(velocity, box_level, turned)
    return force_call(box_level.shape, psi, turned, owner_list, stepped)


def solution(mesh):
    placed = (
        P(None, "gx", "gy", "gz"),
        P(("gx", "gy", "gz"), None, None),
        P(("gx", "gy", "gz"), None),
        P(("gx", "gy", "gz")),
    )
    return jax.shard_map(
        local,
        mesh=mesh,
        in_specs=placed,
        out_specs=(
            P(None, "gx", "gy", "gz"),
            P(("gx", "gy", "gz"), None, None),
            P(("gx", "gy", "gz"), None, None),
        ),
        check_vma=False,
    )
```

```python
import functools
import math

import jax
import jax.numpy as jnp
from jax import lax
from jax.experimental import pallas as pl
from jax.experimental.pallas import tpu as pltpu
from jax.sharding import PartitionSpec as P

ITERS = 12

box_step = 0.25
pseudo_step = 0.3
weno_floor = 1e-06
band_width = 1.5
tension = 2.0
grid_step = 0.2
viscosity = 0.1
normal_floor = 0.5
tiny = 1.1754944e-38

FETCH, GATHER, ADVECT, SECTION, BEND, PUSH, DEPOSIT = 4, 2, 4, 5, 4, 4, 4

MESH = pl.DeviceIdType.MESH


def iota(shape, dim):
    return lax.broadcasted_iota(jnp.int32, shape, dim)


def blend(a, b, c, e, f):
    d1, d2, d3, d4 = a - b, b - c, c - e, e - f
    twice, thrice = 3.0 * d2, 3.0 * d3
    x1, x2, x3 = d1 - d2, d2 - d3, d3 - d4
    y1, y2, y3 = d1 - twice, d2 + d3, thrice - d4
    a1, a2, a3 = [
        (4.0 * weno_floor + (y * y + 13.0 / 3.0 * (x * x))) ** 2
        for x, y in ((x1, y1), (x2, y2), (x3, y3))
    ]
    n1, n2, n3 = a2 * a3, a1 * (6.0 * a3), a1 * (3.0 * a2)
    q1 = 2.0 * d1 - 5.0 * d2
    q2 = d2 + 2.0 * d3
    q3 = d4 - 4.0 * d3
    return c + (n1 * q1 - n2 * q2 + n3 * q3) / (6.0 * (n1 + n2 + n3))


class Box:
    def __init__(self, edge, rows, lanes):
        self.edge, self.rows, self.lanes = edge, rows, lanes
        self.row, self.lane = iota((rows, lanes), 0), iota((rows, lanes), 1)
        j_at, k_at = self.row % edge, self.lane % edge
        self.j_first, self.j_last = j_at == 0, j_at == edge - 1
        self.k_first, self.k_last = k_at == 0, k_at == edge - 1
        self.groups = rows // edge
        self.per = lanes // edge
        self.halves = edge // 8

    def prev_j(self, x):
        return jnp.where(self.j_first, x, pltpu.roll(x, 1, 0))

    def next_j(self, x):
        return jnp.where(self.j_last, x, pltpu.roll(x, self.rows - 1, 0))

    def prev_k(self, x):
        return jnp.where(self.k_first, x, pltpu.roll(x, 1, 1))

    def next_k(self, x):
        return jnp.where(self.k_last, x, pltpu.roll(x, self.lanes - 1, 1))

    def swap_blocks(self, x):
        block = self.lane // self.edge
        for b in (1, 2, 4):
            low = jnp.logical_and((self.row & b) != 0, (block & b) == 0)
            high = jnp.logical_and((self.row & b) == 0, (block & b) != 0)
            down = pltpu.roll(pltpu.roll(x, b, 0), self.lanes - self.edge * b, 1)
            up = pltpu.roll(pltpu.roll(x, self.rows - b, 0), self.edge * b, 1)
            x = jnp.where(low, down, jnp.where(high, up, x))
        return x


def fetch_levels(box, native, lev):
    edge, per = box.edge, box.per

    def fetch(i, carry):
        pieces = [
            native[h, pl.ds(g * per * edge + i, per, stride=edge), :]
            for g in range(box.groups)
            for h in range(box.halves)
        ]
        lev[i] = box.swap_blocks(jnp.concatenate(pieces, axis=0))
        return carry

    lax.fori_loop(0, edge, fetch, 0, unroll=FETCH)


def gather_motion(box, corners, v_ref, mot):
    edge, per, lanes = box.edge, box.per, box.lanes
    slot_lane = iota((edge, lanes), 1) // edge
    for g in range(box.groups):
        places = [[corners[d, g * per + s] for d in range(3)] for s in range(per)]
        turns = [lax.rem(s * edge + lanes - places[s][2], lanes) for s in range(per)]

        def gather(i, carry, g=g, places=places, turns=turns):
            for c in range(3):
                acc = jnp.zeros((edge, lanes), jnp.float32)
                for s in range(per):
                    block = v_ref[c, places[s][0] + i, pl.ds(places[s][1], edge), :]
                    acc = jnp.where(slot_lane == s, pltpu.roll(block, turns[s], 1), acc)
                mot[c, i, pl.ds(g * edge, edge), :] = acc
            return carry

        lax.fori_loop(0, edge, gather, 0, unroll=GATHER)


def advect_levels(box, lev, slope, mot, psa, gain):
    edge = box.edge

    def rise(i, carry):
        slope[i + 3] = lev[i + 1] - lev[i]
        return carry

    zero = jnp.zeros_like(lev[0])
    for n in range(3):
        slope[n] = zero
    lax.fori_loop(0, edge - 1, rise, 0, unroll=5)
    for n in range(3):
        slope[edge + 2 + n] = slope[edge + 1]

    def advect(i, carry):
        here = lev[i]
        change = jnp.zeros_like(here)
        for d in range(3):
            if d == 0:
                slopes = [slope[i + n] for n in range(6)]
            else:
                back, ahead = (box.prev_j, box.next_j) if d == 1 else (box.prev_k, box.next_k)
                mid = here - back(here)
                b1 = back(mid)
                f1 = ahead(mid)
                f2 = ahead(f1)
                slopes = [back(b1), b1, mid, f1, f2, ahead(f2)]
            speed = mot[d, i]
            pos = speed > 0.0
            picks = [jnp.where(pos, slopes[n], slopes[5 - n]) for n in range(5)]
            change = change + speed * blend(*picks)
        out = here - box_step * change
        psa[i] = out
        gain[i] = pseudo_step * out * lax.rsqrt(out * out + 1.0)
        return carry

    lax.fori_loop(0, edge, advect, 0, unroll=ADVECT)


def reinitialize(box, psa, psb, gain):
    edge = box.edge

    def sweep(src, dst):
        for i in range(edge):
            cur = src[i]
            rate = gain[i]
            sign = jnp.where(rate > 0.0, 1.0, -1.0)
            signed = sign * cur
            total = None
            for lo, hi in (
                (src[max(i - 1, 0)], src[min(i + 1, edge - 1)]),
                (box.prev_j(cur), box.next_j(cur)),
                (box.prev_k(cur), box.next_k(cur)),
            ):
                rise = jnp.maximum(signed - jnp.minimum(sign * lo, sign * hi), 0.0)
                total = rise * rise if total is None else total + rise * rise
            root = total * lax.rsqrt(jnp.maximum(total, tiny))
            dst[i] = cur - rate * (root - 1.0)

    def two_sweeps(n, carry):
        sweep(psa, psb)
        sweep(psb, psa)
        return carry

    lax.fori_loop(0, ITERS // 2, two_sweeps, 0)


def pack_z(src, dst, xs, ys, lanes):
    group = iota((ys, lanes), 1) // 4

    def step(x, accs):
        shift = 4 * x + 1
        return tuple(
            jnp.where(group == x, pltpu.roll(src[c, x], shift, 1), accs[c]) for c in range(3)
        )

    accs = lax.fori_loop(
        0, xs, step, tuple(jnp.zeros((ys, lanes), jnp.float32) for _ in range(3)), unroll=8
    )
    for c in range(3):
        dst[c] = accs[c]


def step_kernel(
    sizes, corners, v_hbm, lev_hbm, o_hbm, psi_hbm,
    vel, out, psi_ref, pred, xrecv, ysend, yrecv, zsend, zrecv, comb, lev, slope, mot, psb, gain, native,
    local_sem, lev_sem, out_sem, psi_sem, send_sem, recv_sem,
):
    _, xs, ys, lanes = v_hbm.shape
    box = Box(*lev.shape)
    levels = [
        pltpu.make_async_copy(lev_hbm.at[:, pl.ds(h * lanes, lanes)], native.at[h], lev_sem.at[h])
        for h in range(box.halves)
    ]
    for part in levels:
        part.start()
    load = pltpu.make_async_copy(v_hbm, vel, local_sem)
    load.start()
    ups, downs = [], []
    for axis in ("gx", "gy", "gz"):
        me, n = lax.axis_index(axis), sizes[axis]
        ups.append({axis: lax.rem(me + 1, n)})
        downs.append({axis: lax.rem(me + n - 1, n)})
    barrier = pltpu.get_barrier_semaphore()
    for target in ups + downs:
        pl.semaphore_signal(barrier, inc=1, device_id=target, device_id_type=MESH)
    for part in levels:
        part.wait()
    fetch_levels(box, native, lev)
    load.wait()

    def pack(r, src):
        for c in range(3):
            ysend[r, 0, c] = src[c, :, ys - 1, :]
            ysend[r, 1, c] = src[c, :, 0, :]
        pack_z(src, zsend.at[r], xs, ys, lanes)

    def exchange(r, src):
        copies = []

        def send(n, src, dst, target):
            copy = pltpu.make_async_remote_copy(
                src_ref=src,
                dst_ref=dst,
                send_sem=send_sem.at[r, n],
                recv_sem=recv_sem.at[r, n],
                device_id=target,
                device_id_type=MESH,
            )
            copy.start()
            copies.append(copy)

        send(0, src.at[:, xs - 1], xrecv.at[r, 0], ups[0])
        send(1, src.at[:, 0], xrecv.at[r, 1], downs[0])
        send(2, ysend.at[r, 0], yrecv.at[r, 0], ups[1])
        send(3, ysend.at[r, 1], yrecv.at[r, 1], downs[1])
        send(4, zsend.at[r], zrecv.at[r, 0], ups[2])
        send(5, zsend.at[r], zrecv.at[r, 1], downs[2])
        return copies

    lane = iota((ys, lanes), 1)
    row = iota((ys, lanes), 0)
    quarter = lane % 4

    half = xs // 2

    def store(n):
        part = pl.ds(n * half, half)
        return pltpu.make_async_copy(out.at[:, part], o_hbm.at[:, part], out_sem.at[n])

    def section(r, src, emit, done):
        for c in range(3):
            comb[c] = jnp.where(
                quarter == 0,
                pltpu.roll(zrecv[r, 1, c], lanes - 1, 1),
                pltpu.roll(zrecv[r, 0, c], 1, 1),
            )

        def plane(x, before, after):
            centre = [src[c, x] for c in range(3)]
            for c in range(3):
                mid = centre[c]
                x_lo, x_hi = before(c), after(c)
                y_lo = jnp.where(row == 0, yrecv[r, 0, c, pl.ds(x, 1), :], pltpu.roll(mid, 1, 0))
                y_hi = jnp.where(
                    row == ys - 1, yrecv[r, 1, c, pl.ds(x, 1), :], pltpu.roll(mid, ys - 1, 0)
                )
                halo = pltpu.roll(comb[c], lanes - 1 - 4 * x, 1)
                z_lo = jnp.where(lane == 0, halo, pltpu.roll(mid, 1, 1))
                z_hi = jnp.where(lane == lanes - 1, halo, pltpu.roll(mid, lanes - 1, 1))
                spread = (x_hi + x_lo) + (y_hi + y_lo) + (z_hi + z_lo) - 6.0 * mid
                advect = (
                    centre[0] * (x_hi - x_lo) + centre[1] * (y_hi - y_lo) + centre[2] * (z_hi - z_lo)
                )
                emit(c, x, mid + grid_step * (viscosity * spread - 0.5 * advect))

        def step(x, carry):
            plane(x, lambda c: src[c, x - 1], lambda c: src[c, x + 1])
            return carry

        plane(0, lambda c: xrecv[r, 0, c], lambda c: src[c, 1])
        lax.fori_loop(1, half, step, 0, unroll=SECTION)
        done(0)
        lax.fori_loop(half, xs - 1, step, 0, unroll=SECTION)
        plane(xs - 1, lambda c: src[c, xs - 2], lambda c: xrecv[r, 1, c])
        done(1)

    def first(c, x, value):
        pred[c, x] = value

    def second(c, x, value):
        out[c, x] = 0.5 * (vel[c, x] + value)

    pack(0, vel)
    pl.semaphore_wait(barrier, 6)
    copies = exchange(0, vel)
    gather_motion(box, corners, vel, mot)
    advect_levels(box, lev, slope, mot, psi_ref, gain)
    for copy in copies:
        copy.wait()
    section(0, vel, first, lambda n: None)
    pack(1, pred)
    copies = exchange(1, pred)
    reinitialize(box, psi_ref, psb, gain)
    keep = pltpu.make_async_copy(psi_ref, psi_hbm, psi_sem)
    keep.start()
    for copy in copies:
        copy.wait()
    section(1, pred, second, lambda n: store(n).start())
    store(0).wait()
    store(1).wait()
    keep.wait()


def step_call(velocity, box_level, corners):
    sizes = {axis: lax.axis_size(axis) for axis in ("gx", "gy", "gz")}
    _, xs, ys, lanes = velocity.shape
    slots, edge, plane = box_level.shape
    rows = slots * edge * plane // (edge * lanes)
    vmem = pltpu.VMEM
    f32 = jnp.float32
    return pl.pallas_call(
        functools.partial(step_kernel, sizes),
        out_shape=(
            jax.ShapeDtypeStruct(velocity.shape, f32),
            jax.ShapeDtypeStruct((edge, rows, lanes), f32),
        ),
        in_specs=[
            pl.BlockSpec(memory_space=pltpu.SMEM),
            pl.BlockSpec(memory_space=pl.ANY),
            pl.BlockSpec(memory_space=pl.ANY),
        ],
        out_specs=(pl.BlockSpec(memory_space=pl.ANY), pl.BlockSpec(memory_space=pl.ANY)),
        scratch_shapes=[
            vmem(velocity.shape, f32),
            vmem(velocity.shape, f32),
            vmem((edge, rows, lanes), f32),
            vmem(velocity.shape, f32),
            vmem((2, 2, 3, ys, lanes), f32),
            vmem((2, 2, 3, xs, lanes), f32),
            vmem((2, 2, 3, xs, lanes), f32),
            vmem((2, 3, ys, lanes), f32),
            vmem((2, 2, 3, ys, lanes), f32),
            vmem((3, ys, lanes), f32),
            vmem((edge, rows, lanes), f32),
            vmem((edge + 5, rows, lanes), f32),
            vmem((3, edge, rows, lanes), f32),
            vmem((edge, rows, lanes), f32),
            vmem((edge, rows, lanes), f32),
            vmem((plane // lanes, slots * edge, lanes), f32),
            pltpu.SemaphoreType.DMA(()),
            pltpu.SemaphoreType.DMA((plane // lanes,)),
            pltpu.SemaphoreType.DMA((2,)),
            pltpu.SemaphoreType.DMA(()),
            pltpu.SemaphoreType.DMA((2, 6)),
            pltpu.SemaphoreType.DMA((2, 6)),
        ],
        compiler_params=pltpu.CompilerParams(collective_id=0, has_side_effects=True),
    )(corners, velocity, box_level.reshape(slots * edge, plane))


def force_kernel(
    corners, owners, psi, step_hbm, o_hbm, set_hbm, ben_hbm,
    o_ref, force, part, nrm, native_a, native_b, sem, out_sem, small_sem,
):
    load = pltpu.make_async_copy(step_hbm, o_ref, sem)
    load.start()
    box = Box(*psi.shape)
    edge, per, groups, lanes = box.edge, box.per, box.groups, box.lanes

    def write(ref, i, value):
        value = box.swap_blocks(value)
        for g in range(groups):
            for h in range(box.halves):
                at = g * edge + h * 8
                ref[h, pl.ds(g * per * edge + i, per, stride=edge), :] = value[at : at + 8]

    alive = jnp.zeros((box.rows, lanes), jnp.float32)
    owner_at = (box.row // edge) * per + box.lane // edge
    for s in range(groups * per):
        alive = jnp.where(owner_at == s, jnp.where(owners[s] >= 0, 1.0, 0.0), alive)

    def bend(i, carry):
        cur = psi[i]
        c0 = 0.5 * (psi[jnp.minimum(i + 1, edge - 1)] - psi[jnp.maximum(i - 1, 0)])
        c1 = 0.5 * (box.next_j(cur) - box.prev_j(cur))
        c2 = 0.5 * (box.next_k(cur) - box.prev_k(cur))
        inverse = lax.rsqrt(jnp.maximum(c0 * c0 + c1 * c1 + c2 * c2, normal_floor * normal_floor))
        n1, n2 = c1 * inverse, c2 * inverse
        nrm[i] = c0 * inverse
        part[i] = 0.5 * (box.next_j(n1) - box.prev_j(n1)) + 0.5 * (box.next_k(n2) - box.prev_k(n2))
        force[0, i] = c0
        force[1, i] = c1
        force[2, i] = c2
        return carry

    lax.fori_loop(0, edge, bend, 0, unroll=BEND)

    def push(i, carry):
        level = psi[i] * alive
        curve = (
            part[i] + 0.5 * (nrm[jnp.minimum(i + 1, edge - 1)] - nrm[jnp.maximum(i - 1, 0)])
        ) * alive
        write(native_a, i, level)
        write(native_b, i, curve)
        ratio = level * (1.0 / band_width)
        scale = grid_step * tension / (band_width * math.sqrt(math.pi))
        strength = scale * curve * jnp.exp(-(ratio * ratio)) * alive
        for d in range(3):
            force[d, i] = force[d, i] * strength
        return carry

    lax.fori_loop(0, edge, push, 0, unroll=PUSH)
    stores = []
    for h in range(box.halves):
        part_h = pl.ds(h * lanes, lanes)
        stores.append(pltpu.make_async_copy(native_a.at[h], set_hbm.at[:, part_h], small_sem.at[0, h]))
        stores.append(pltpu.make_async_copy(native_b.at[h], ben_hbm.at[:, part_h], small_sem.at[1, h]))
    for copy in stores:
        copy.start()

    load.wait()
    wide = iota((edge, lanes), 1)

    def deposit_slot(n, carry):
        g, s = n // per, n % per
        ax, ay, az = corners[0, n], corners[1, n], corners[2, n]
        turn = lax.rem(az + lanes - s * edge, lanes)
        inside = jnp.logical_and(wide >= az, wide < az + edge)
        first_row = pl.multiple_of(g * edge, edge)

        for i in range(0, edge, DEPOSIT):
            spots = [(c, i + t) for t in range(DEPOSIT) for c in range(3)]
            blocks = [pltpu.roll(force[c, q, pl.ds(first_row, edge), :], turn, 1) for c, q in spots]
            olds = [o_ref[c, ax + q, pl.ds(ay, edge), :] for c, q in spots]
            news = [old + jnp.where(inside, block, 0.0) for old, block in zip(olds, blocks)]
            for (c, q), new in zip(spots, news):
                o_ref[c, ax + q, pl.ds(ay, edge), :] = new
        return carry

    lax.fori_loop(0, groups * per, deposit_slot, 0)
    for c in range(3):
        stores.append(pltpu.make_async_copy(o_ref.at[c], o_hbm.at[c], out_sem.at[c]))
        stores[-1].start()
    for copy in stores:
        copy.wait()


def force_call(shapes, psi, corners, owner_list, stepped):
    slots, edge, plane = shapes
    rows, lanes = psi.shape[1:]
    flat = (slots * edge, plane)
    f32 = jnp.float32
    whole = pl.BlockSpec(memory_space=pltpu.VMEM)
    smem = pl.BlockSpec(memory_space=pltpu.SMEM)
    field = pltpu.VMEM((edge, rows, lanes), f32)
    native = pltpu.VMEM((plane // lanes, slots * edge, lanes), f32)
    result, settled, bending = pl.pallas_call(
        force_kernel,
        out_shape=(
            jax.ShapeDtypeStruct(stepped.shape, f32),
            jax.ShapeDtypeStruct(flat, f32),
            jax.ShapeDtypeStruct(flat, f32),
        ),
        in_specs=[smem, smem, whole, pl.BlockSpec(memory_space=pl.ANY)],
        out_specs=(pl.BlockSpec(memory_space=pl.ANY),) * 3,
        scratch_shapes=[
            pltpu.VMEM(stepped.shape, f32),
            pltpu.VMEM((3, edge, rows, lanes), f32),
            field,
            field,
            native,
            native,
            pltpu.SemaphoreType.DMA(()),
            pltpu.SemaphoreType.DMA((3,)),
            pltpu.SemaphoreType.DMA((2, plane // lanes)),
        ],
    )(corners, owner_list, psi, stepped)
    return result, settled.reshape(shapes), bending.reshape(shapes)


def local(velocity, box_level, corners, owner_list):
    turned = corners.T
    stepped, psi = step_call(velocity, box_level, turned)
    return force_call(box_level.shape, psi, turned, owner_list, stepped)


def solution(mesh):
    placed = (
        P(None, "gx", "gy", "gz"),
        P(("gx", "gy", "gz"), None, None),
        P(("gx", "gy", "gz"), None),
        P(("gx", "gy", "gz")),
    )
    return jax.shard_map(
        local,
        mesh=mesh,
        in_specs=placed,
        out_specs=(
            P(None, "gx", "gy", "gz"),
            P(("gx", "gy", "gz"), None, None),
            P(("gx", "gy", "gz"), None, None),
        ),
        check_vma=False,
    )
```
